32 devices in a mesh: section: 2 (over core), expert: 4 (over y, x), tensor: 4 (over z).
Axes of the slice: x: 2, y: 2, z: 4, core: 2. Of those that a mesh axis runs over, the one named last changes fastest.
Arguments:
- inputs: float32 [1, 788, 768], P(None, 'expert'), may hold values from -6 to 6
- cotangent: float32 [1, 788, 768], P(None, 'expert'), may hold values from -6 to 6
- norm_scale: float32 [2, 2, 768], P('section'), may hold values from 0.5 to 1.5
- norm_shift: float32 [2, 2, 768], P('section'), may hold values from -3 to 3
- proj_weight: bfloat16 [2, 768, 3, 768], P('section', None, None, 'tensor'), may hold values from -0.21875 to 0.21875
- proj_bias: float32 [2, 2, 768], P('section', None, 'tensor'), may hold values from -3 to 3
- attn_weight: bfloat16 [2, 768, 768], P('section', 'tensor'), may hold values from -0.75 to 0.75
- attn_bias: float32 [2, 768], P('section'), may hold values from -3 to 3
- expert_in: bfloat16 [2, 4, 768, 3072], P('section', 'expert', None, 'tensor'), may hold values from -0.21875 to 0.21875
- expert_in_bias: float32 [2, 4, 3072], P('section', 'expert', 'tensor'), may hold values from -3 to 3
- expert_out: bfloat16 [2, 4, 3072, 768], P('section', 'expert', 'tensor'), may hold values from -0.109375 to 0.109375
- expert_out_bias: float32 [2, 4, 768], P('section', 'expert'), may hold values from -3 to 3
- routes: int32 [2, 1, 788, 2], P('section', None, 'expert'), may hold values from 0 to 3, all different within a row; in each aligned block of 197 rows (0 to 196, 197 to 393, ..., all dimensions but the last counted through in order) at most 148 rows name the same one
- gate_weights: float32 [2, 1, 788, 2], P('section', None, 'expert'), may hold values from 0.1 to 1
Outputs:
- section_out: float32 [2, 1, 788, 768], P('section', None, 'expert')
- section_in_grad: float32 [2, 1, 788, 768], P('section', None, 'expert')
- grad_norm_scale: float32 [2, 2, 768], P('section')
- grad_norm_shift: float32 [2, 2, 768], P('section')
- grad_proj_weight: float32 [2, 768, 3, 768], P('section', None, None, 'tensor')
- grad_proj_bias: float32 [2, 2, 768], P('section', None, 'tensor')
- grad_attn_weight: float32 [2, 768, 768], P('section', 'tensor')
- grad_attn_bias: float32 [2, 768], P('section')
- grad_expert_in: float32 [2, 4, 768, 3072], P('section', 'expert', None, 'tensor')
- grad_expert_in_bias: float32 [2, 4, 3072], P('section', 'expert', 'tensor')
- grad_expert_out: float32 [2, 4, 3072, 768], P('section', 'expert', 'tensor')
- grad_expert_out_bias: float32 [2, 4, 768], P('section', 'expert')
The draws below stay inside these ranges and needn't reach their ends.
Inputs may be any that keep to these rules, and one draw needn't show every extreme that they name: `routes`: each row names 2 different experts. In the rows of one index of the expert axis for one section and micro-batch, no expert is named more than 148 times, and in every draw some expert is named exactly 148 times there.
All inputs are finite; a program needn't handle non-finite values.
Results may differ from the reference program's by a relative error of at most 0.015.
Values may be sent and summed in bfloat16 or wider, within the bound.
A program may use at most 128 MiB of HBM per device.

```python
import math
import jax
import jax.numpy as jnp
import numpy as np
from jax import lax

D = 768
HEADS = 12
HEAD_DIM = 64
HIDDEN_SIZE = 3072
SEQ = 197
TOPK = 2
MICRO = 1
TOK_DEV = 197
TOKENS = 788
IMAGES = 4
EXPERTS = 4
CAP = 148
N_SECTION = 2


def block_levels(own_key, shape, cuts, low, largest):
    def one(dim, parts):
        draws = jax.random.uniform(jax.random.fold_in(jax.random.fold_in(own_key, 6), dim), (parts,), jnp.float32, low / len(cuts), largest / len(cuts))
        return jnp.repeat(jnp.exp(draws), shape[dim] // parts).reshape((-1,) + (1,) * (len(shape) - dim - 1))

    factor_of = one(*cuts[0])
    for cut in cuts[1:]:
        factor_of = factor_of * one(*cut)
    return factor_of


def shared_out(rng, own, number, rows, amount, top, limit, lean):
    ranking = jax.random.permutation(rng, amount)
    packed, ordinary = portions_of(amount, rows * top, limit, lean, True), portions_of(amount, rows * top, limit, lean, False)
    places = jnp.arange(amount)

    def named(lengths, offset_by):
        used = int((lengths > 0).sum())
        fixed = max(1, used // 4)
        passed = fixed + (places - fixed + offset_by * (used - fixed)) % max(1, amount - fixed)
        return jnp.zeros((amount,), jnp.int32).at[ranking[jnp.where(places < fixed, places, passed)]].set(jnp.asarray(lengths, jnp.int32))

    lengths = jnp.where(number % 4 == 0, named(packed, number // 4), named(ordinary, number - number // 4 - 1))
    mixed = jax.random.permutation(jax.random.fold_in(own, 3), amount)
    source_of, sink = mixed[0:amount // 2 * 2:2], mixed[1:amount // 2 * 2:2]
    margin = jnp.minimum(lengths[source_of] - 1, limit - lengths[sink]) // 2
    margin = jnp.where((source_of == ranking[0]) | (sink == ranking[0]) | (lengths[sink] == 0), 0, jnp.maximum(margin, 0))
    passed = jax.random.randint(jax.random.fold_in(own, 4), (amount // 2,), 0, 1 << 20) % (margin + 1)
    lengths = lengths.at[source_of].add(-passed).at[sink].add(passed)
    members = jnp.searchsorted(jnp.cumsum(lengths), jnp.arange(rows * top), side="right").astype(jnp.int32)
    grid = members.reshape(top, rows).T
    grid = grid[jax.random.permutation(jax.random.fold_in(own, 1), rows)]
    offset_by = jax.random.randint(jax.random.fold_in(own, 2), (rows, 1), 0, top)
    return jnp.take_along_axis(grid, (jnp.arange(top)[None, :] + offset_by) % top, axis=1)


def portions_of(number_of, total, most, slope, full):
    portions = [(1 << 20) // math.isqrt(grade ** slope) + 1 for grade in range(1, number_of + 1)]
    largest = most if full else min(most, max(-(-total // number_of), total * portions[0] // sum(portions)))
    least = 1 if total - largest >= number_of - 1 else 0
    given, spare = [largest] + [least] * (number_of - 1), total - largest - least * (number_of - 1)
    while spare > 0:
        movable = [i for i in range(1, number_of) if given[i] < largest] or [i for i in range(1, number_of) if given[i] < most]
        whole, left = sum([portions[i] for i in movable]), spare
        for i in movable:
            more = min(most - given[i], max(1, left * portions[i] // whole), spare)
            given[i] = given[i] + more
            spare = spare - more
    return np.array(given)


def bell_draw(key, shape, spread, most, pieces=(), held_as=jnp.bfloat16):
    loudness = block_levels(key, shape, pieces, -0.22, 0.18) if pieces else 1.0
    entries = jax.random.normal(key, shape, jnp.float32) * spread * loudness
    return jnp.minimum(jnp.maximum(entries, -most), most).astype(held_as)


def setup_inputs(seed: int = 0) -> dict:
    streams_of = jax.random.split(jax.random.key(seed), 15)
    inputs = bell_draw(streams_of[0], (MICRO, TOKENS, D), 1.0, 6.0, ((1, 4),), jnp.float32)
    cotangent = bell_draw(streams_of[1], (MICRO, TOKENS, D), 1.0, 6.0, ((1, 4),), jnp.float32)
    norm_scale = jnp.clip(1.0 + 0.1 * jax.random.normal(streams_of[2], (N_SECTION, 2, D), jnp.float32), 0.5, 1.5)
    norm_shift = bell_draw(streams_of[3], (N_SECTION, 2, D), 0.3, 3.0, ((0, 2),), jnp.float32)
    proj_weight = bell_draw(streams_of[4], (N_SECTION, D, 3, D), D ** -0.5, 0.21875, ((0, 2), (3, 4)))
    proj_bias = bell_draw(streams_of[5], (N_SECTION, 2, D), 0.5, 3.0, ((0, 2), (2, 4)), jnp.float32)
    attn_weight = bell_draw(streams_of[6], (N_SECTION, D, D), (D // 12) ** -0.5, 0.75, ((0, 2), (1, 4)))
    attn_bias = bell_draw(streams_of[7], (N_SECTION, D), 0.5, 3.0, ((0, 2),), jnp.float32)
    expert_in = bell_draw(streams_of[8], (N_SECTION, EXPERTS, D, HIDDEN_SIZE), D ** -0.5, 0.21875, ((0, 2), (1, 4), (3, 4)))
    expert_in_bias = bell_draw(streams_of[9], (N_SECTION, EXPERTS, HIDDEN_SIZE), 0.5, 3.0, ((0, 2), (1, 4), (2, 4)), jnp.float32)
    expert_out = bell_draw(streams_of[10], (N_SECTION, EXPERTS, HIDDEN_SIZE, D), HIDDEN_SIZE ** -0.5, 0.109375, ((0, 2), (1, 4), (2, 4)))
    expert_out_bias = bell_draw(streams_of[11], (N_SECTION, EXPERTS, D), 0.5, 3.0, ((0, 2), (1, 4)), jnp.float32)
    routes_keys = jax.random.split(jax.random.fold_in(streams_of[12], 1), N_SECTION * MICRO * TOKENS // TOK_DEV)
    routes_turns = jax.random.permutation(jax.random.fold_in(streams_of[12], 3), N_SECTION * MICRO * TOKENS // TOK_DEV)
    routes = jax.vmap(lambda own, number: shared_out(jax.random.fold_in(streams_of[12], 2), own, number, TOK_DEV, EXPERTS, TOPK, CAP, 2))(routes_keys, routes_turns).reshape((N_SECTION, MICRO, TOKENS, TOPK))
    gate_weights = jnp.clip(0.1 + 0.9 * jax.random.uniform(streams_of[13], (N_SECTION, MICRO, TOKENS, TOPK), jnp.float32) ** block_levels(streams_of[13], (N_SECTION, MICRO, TOKENS, TOPK), ((0, 2), (2, 4)), -0.2, 0.2), 0.1, 1.0)
    return dict(inputs=inputs, cotangent=cotangent, norm_scale=norm_scale, norm_shift=norm_shift, proj_weight=proj_weight, proj_bias=proj_bias, attn_weight=attn_weight, attn_bias=attn_bias, expert_in=expert_in, expert_in_bias=expert_in_bias, expert_out=expert_out, expert_out_bias=expert_out_bias, routes=routes, gate_weights=gate_weights)


NORM_EPSILON = 1e-06
GELU_FACTOR = 0.7978845608028654
CUBIC_TERM = 0.044715

def gelu_value(pre_act):
    inner_arg = GELU_FACTOR * (pre_act + CUBIC_TERM * pre_act * pre_act * pre_act)
    return 0.5 * pre_act * (1.0 + jnp.tanh(inner_arg))

def gelu_slope(pre_act):
    tangent = jnp.tanh(GELU_FACTOR * (pre_act + CUBIC_TERM * pre_act * pre_act * pre_act))
    return 0.5 * (1.0 + tangent) + 0.5 * pre_act * (1.0 - tangent * tangent) * GELU_FACTOR * (1.0 + 3.0 * CUBIC_TERM * pre_act * pre_act)

def layer_norm(values, scale_row, shift_row):
    average = lax.optimization_barrier(jnp.mean(values, axis=-1, keepdims=True))
    centred = values - average
    variance = lax.optimization_barrier(jnp.mean(centred * centred, axis=-1, keepdims=True))
    inv_std = lax.rsqrt(variance + NORM_EPSILON)
    normed = centred * inv_std
    return (normed * scale_row + shift_row, normed, inv_std)

def norm_back(grad_normed, normed, inv_std, scale_row):
    scaled = grad_normed * scale_row
    return (scaled - lax.optimization_barrier(jnp.mean(scaled, axis=-1, keepdims=True)) - normed * lax.optimization_barrier(jnp.mean(scaled * normed, axis=-1, keepdims=True))) * inv_std

def slot_table(route_rows, experts, capacity):
    flat_ids = route_rows.reshape(-1).astype(jnp.int32)
    onehot = (flat_ids[:, None] == jnp.arange(experts, dtype=jnp.int32)[None, :]).astype(jnp.int32)
    before = jnp.cumsum(onehot, axis=0) - onehot
    position = lax.optimization_barrier(jnp.sum(before * onehot, axis=1)).astype(jnp.int32)
    return flat_ids * capacity + position

def to_float(values):
    return values.astype(jnp.float32)

def fill_slots(slot_ids, block_rows):

    def one_block(id_row, value_rows):
        return jnp.zeros((EXPERTS * CAP, value_rows.shape[-1]), value_rows.dtype).at[id_row].set(value_rows)
    return jax.vmap(one_block)(slot_ids, block_rows)

def to_experts(buffer):
    width_last = buffer.shape[-1]
    return buffer.reshape(EXPERTS, EXPERTS, CAP, width_last).transpose(1, 0, 2, 3).reshape(EXPERTS, EXPERTS * CAP, width_last)

def to_blocks(by_expert):
    width_last = by_expert.shape[-1]
    return by_expert.reshape(EXPERTS, EXPERTS, CAP, width_last).transpose(1, 0, 2, 3).reshape(EXPERTS, EXPERTS * CAP, width_last)

def pick_slots(table, slot_ids):
    return jax.vmap(lambda table_rows, id_row: table_rows[id_row])(table, slot_ids)

def attend(query_rows, key_rows, value_rows):
    scores = jnp.einsum('ishe,ithe->ihst', to_float(query_rows), to_float(key_rows)) * HEAD_DIM ** (-0.5)
    log_total = jnp.log(lax.optimization_barrier(jnp.sum(jnp.exp(scores), axis=-1)))
    prob_rows = jnp.exp(scores - log_total[..., None]).astype(jnp.bfloat16)
    attn_mixed = jnp.einsum('ihst,ithe->ishe', to_float(prob_rows), to_float(value_rows)).astype(jnp.bfloat16)
    return (attn_mixed, log_total)

def attend_back(query_rows, key_rows, value_rows, attn_mixed, log_total, grad_mixed):
    scale_factor = HEAD_DIM ** (-0.5)
    scores = jnp.einsum('ishe,ithe->ihst', to_float(query_rows), to_float(key_rows)) * scale_factor
    prob_f = jnp.exp(scores - log_total[..., None])
    prob_rows = prob_f.astype(jnp.bfloat16)
    grad_values = jnp.einsum('ihst,ishe->ithe', to_float(prob_rows), to_float(grad_mixed))
    grad_probs = jnp.einsum('ishe,ithe->ihst', to_float(grad_mixed), to_float(value_rows))
    row_delta = jnp.einsum('ishe,ishe->ihs', to_float(grad_mixed), to_float(attn_mixed))
    grad_scores = (prob_f * (grad_probs - row_delta[..., None]) * scale_factor).astype(jnp.bfloat16)
    grad_query = jnp.einsum('ihst,ithe->ishe', to_float(grad_scores), to_float(key_rows))
    grad_keys = jnp.einsum('ihst,ishe->ithe', to_float(grad_scores), to_float(query_rows))
    return (grad_query, grad_keys, grad_values)

def forward_block(inputs, weights, route_rows, gate_rows):
    norm_scale, norm_shift, proj_weight, proj_bias, attn_weight, attn_bias, expert_in, expert_in_bias, expert_out, expert_out_bias = weights
    head_shape = (IMAGES, SEQ, HEADS, HEAD_DIM)
    normed_out, normed_first, inv_first = layer_norm(inputs, norm_scale[0], norm_shift[0])
    normed_a = normed_out.astype(jnp.bfloat16)
    projected = jnp.einsum('rd,dkf->rkf', to_float(normed_a), to_float(proj_weight))
    query_rows = (projected[:, 0] + proj_bias[0]).astype(jnp.bfloat16).reshape(head_shape)
    key_rows = projected[:, 1].astype(jnp.bfloat16).reshape(head_shape)
    value_rows = (projected[:, 2] + proj_bias[1]).astype(jnp.bfloat16).reshape(head_shape)
    attn_mixed, log_total = attend(query_rows, key_rows, value_rows)
    mixed_flat = attn_mixed.reshape(TOKENS, D)
    hidden_res = inputs + (jnp.dot(mixed_flat, attn_weight, preferred_element_type=jnp.float32) + attn_bias)
    normed_out_b, normed_second, inv_second = layer_norm(hidden_res, norm_scale[1], norm_shift[1])
    normed_b = normed_out_b.astype(jnp.bfloat16)
    slot_ids = jax.vmap(lambda rows_here: slot_table(rows_here, EXPERTS, CAP))(route_rows.reshape(EXPERTS, TOK_DEV, TOPK))
    repeated = jnp.repeat(normed_b.reshape(EXPERTS, TOK_DEV, D), TOPK, axis=1)
    by_expert = to_experts(fill_slots(slot_ids, repeated))

    def one_expert(operands):
        rows_here, weight_in, bias_in, weight_out, bias_out = operands
        pre_act = jnp.dot(rows_here, weight_in, preferred_element_type=jnp.float32) + bias_in
        activated = gelu_value(pre_act).astype(jnp.bfloat16)
        result_rows = (jnp.dot(activated, weight_out, preferred_element_type=jnp.float32) + bias_out).astype(jnp.bfloat16)
        return (result_rows, pre_act)
    expert_result, pre_act = lax.map(one_expert, (by_expert, expert_in, expert_in_bias, expert_out, expert_out_bias))
    picked = pick_slots(to_blocks(expert_result), slot_ids)
    branch = lax.optimization_barrier(jnp.sum(gate_rows.reshape(TOKENS, TOPK, 1) * to_float(picked).reshape(TOKENS, TOPK, D), axis=1))
    block_out = hidden_res + branch
    kept_state = (normed_first, inv_first, query_rows, key_rows, value_rows, attn_mixed, log_total, normed_second, inv_second, slot_ids, gate_rows, by_expert, pre_act)
    return (block_out, kept_state)

def backward_block(cotangent, weights, kept_state):
    norm_scale, norm_shift, proj_weight, proj_bias, attn_weight, attn_bias, expert_in, expert_in_bias, expert_out, expert_out_bias = weights
    normed_first, inv_first, query_rows, key_rows, value_rows, attn_mixed, log_total, normed_second, inv_second, slot_ids, gate_rows, by_expert, pre_act = kept_state
    head_shape = (IMAGES, SEQ, HEADS, HEAD_DIM)
    grad_rows = (gate_rows.reshape(TOKENS, TOPK, 1) * cotangent[:, None, :]).astype(jnp.bfloat16).reshape(EXPERTS, TOPK * TOK_DEV, D)
    grad_by_expert = to_experts(fill_slots(slot_ids, grad_rows))

    def one_expert_back(operands):
        rows_here, pre_here, grad_here, weight_in, weight_out = operands
        activated = gelu_value(pre_here).astype(jnp.bfloat16)
        grad_weight_out = jnp.dot(activated.T, grad_here, preferred_element_type=jnp.float32)
        grad_bias_out = lax.optimization_barrier(jnp.sum(to_float(grad_here), axis=0))
        grad_pre = jnp.dot(grad_here, weight_out.T, preferred_element_type=jnp.float32) * gelu_slope(pre_here)
        grad_bias_in = lax.optimization_barrier(jnp.sum(grad_pre, axis=0))
        grad_pre_b = grad_pre.astype(jnp.bfloat16)
        grad_weight_in = jnp.dot(rows_here.T, grad_pre_b, preferred_element_type=jnp.float32)
        grad_buffer = jnp.dot(grad_pre_b, weight_in.T, preferred_element_type=jnp.float32).astype(jnp.bfloat16)
        return (grad_weight_in, grad_bias_in, grad_weight_out, grad_bias_out, grad_buffer)
    grad_expert_in, grad_expert_in_bias, grad_expert_out, grad_expert_out_bias, grad_buffer = lax.map(one_expert_back, (by_expert, pre_act, grad_by_expert, expert_in, expert_out))
    picked = pick_slots(to_blocks(grad_buffer), slot_ids)
    grad_normed_b = lax.optimization_barrier(jnp.sum(to_float(picked).reshape(TOKENS, TOPK, D), axis=1))
    grad_hidden = cotangent + norm_back(grad_normed_b, normed_second, inv_second, norm_scale[1])
    grad_hidden_b = grad_hidden.astype(jnp.bfloat16)
    grad_attn_bias = lax.optimization_barrier(jnp.sum(grad_hidden, axis=0))
    mixed_flat = attn_mixed.reshape(TOKENS, D)
    grad_attn_weight = jnp.dot(mixed_flat.T, grad_hidden_b, preferred_element_type=jnp.float32)
    grad_mixed = jnp.dot(grad_hidden_b, attn_weight.T, preferred_element_type=jnp.float32).astype(jnp.bfloat16).reshape(head_shape)
    grad_query, grad_keys, grad_values = attend_back(query_rows, key_rows, value_rows, attn_mixed, log_total, grad_mixed)
    query_flat = grad_query.reshape(TOKENS, D)
    key_flat = grad_keys.reshape(TOKENS, D)
    value_flat = grad_values.reshape(TOKENS, D)
    grad_proj_bias = jnp.stack([lax.optimization_barrier(jnp.sum(query_flat, axis=0)), lax.optimization_barrier(jnp.sum(value_flat, axis=0))])
    grad_proj = jnp.stack([query_flat, key_flat, value_flat], axis=1).astype(jnp.bfloat16)
    normed_a = (normed_first * norm_scale[0] + norm_shift[0]).astype(jnp.bfloat16)
    grad_proj_weight = jnp.einsum('rd,rkf->dkf', to_float(normed_a), to_float(grad_proj))
    grad_normed_a = jnp.einsum('rkf,dkf->rd', to_float(grad_proj), to_float(proj_weight))
    grad_input = grad_hidden + norm_back(grad_normed_a, normed_first, inv_first, norm_scale[0])
    grad_norm_scale = jnp.stack([lax.optimization_barrier(jnp.sum(grad_normed_a * normed_first, axis=0)), lax.optimization_barrier(jnp.sum(grad_normed_b * normed_second, axis=0))])
    grad_norm_shift = jnp.stack([lax.optimization_barrier(jnp.sum(grad_normed_a, axis=0)), lax.optimization_barrier(jnp.sum(grad_normed_b, axis=0))])
    grad_parts = (grad_norm_scale, grad_norm_shift, grad_proj_weight, grad_proj_bias, grad_attn_weight, grad_attn_bias, grad_expert_in, grad_expert_in_bias, grad_expert_out, grad_expert_out_bias)
    return (grad_input, grad_parts)

def reference(inputs, cotangent, norm_scale, norm_shift, proj_weight, proj_bias, attn_weight, attn_bias, expert_in, expert_in_bias, expert_out, expert_out_bias, routes, gate_weights):
    params = (norm_scale, norm_shift, proj_weight, proj_bias, attn_weight, attn_bias, expert_in, expert_in_bias, expert_out, expert_out_bias)
    section_outputs = []
    section_kept = []
    current = [inputs[micro_index] for micro_index in range(MICRO)]
    for section_index in range(N_SECTION):
        weights = tuple((member[section_index] for member in params))
        outputs_here = []
        kept_here = []
        for micro_index in range(MICRO):
            block_out, kept_state = forward_block(current[micro_index], weights, routes[section_index, micro_index], gate_weights[section_index, micro_index])
            outputs_here.append(block_out)
            kept_here.append(kept_state)
        section_outputs.append(jnp.stack(outputs_here))
        section_kept.append(kept_here)
        current = outputs_here
    section_grads = [None] * N_SECTION
    input_grads = [None] * N_SECTION
    flowing = [cotangent[micro_index] for micro_index in range(MICRO)]
    for section_index in reversed(range(N_SECTION)):
        weights = tuple((member[section_index] for member in params))
        running = None
        grads_here = []
        for micro_index in range(MICRO):
            grad_input, grad_parts = backward_block(flowing[micro_index], weights, section_kept[section_index][micro_index])
            running = grad_parts if running is None else jax.tree.map(jnp.add, running, grad_parts)
            grads_here.append(grad_input)
        section_grads[section_index] = running
        input_grads[section_index] = jnp.stack(grads_here)
        flowing = grads_here
    stacked = [jnp.stack([section_grads[section_index][member] for section_index in range(N_SECTION)]) for member in range(10)]
    return (jnp.stack(section_outputs), jnp.stack(input_grads), stacked[0], stacked[1], stacked[2], stacked[3], stacked[4], stacked[5], stacked[6], stacked[7], stacked[8], stacked[9])
```

```python
import functools
import itertools

import jax
import jax.numpy as jnp
from jax import lax
from jax.experimental import pallas as pl
from jax.experimental.pallas import tpu as pltpu
from jax.sharding import PartitionSpec as P

HEAD_DIM = 64
SEQ = 197
TOPK = 2


NORM_EPSILON = 1e-06
GELU_FACTOR = 0.7978845608028654
CUBIC_TERM = 0.044715


MESH = pl.DeviceIdType.MESH
ROW_TILE = 16
BF16 = jnp.bfloat16
F32 = jnp.float32


def from_behind(block, axis, distance):
    devices = range(lax.axis_size(axis))
    route = [(i - distance, i) for i in devices if i - distance in devices]
    return lax.ppermute(block, axis, route)


def flat_index(places, sizes):
    total = places[0]
    for place, size in zip(places[1:], sizes[1:]):
        total = total * size + place
    return total


def partners(axes, sizes):
    here = [lax.axis_index(axis) for axis in axes]
    others = []
    for offsets in itertools.product(*[range(size) for size in sizes]):
        if any(offsets):
            there = [
                lax.rem(place + offset, size) if offset else place
                for place, offset, size in zip(here, offsets, sizes)
            ]
            others.append((flat_index(there, sizes), dict(zip(axes, there))))
    return flat_index(here, sizes), others


def greet(others):
    barrier = pltpu.get_barrier_semaphore()
    for _, device in others:
        pl.semaphore_signal(barrier, inc=1, device_id=device, device_id_type=MESH)
    pl.semaphore_wait(barrier, len(others))


def when_active(active, body):
    if active is None:
        body()
    else:
        pl.when(lax.axis_index("section") == active)(body)


def send(source, target, send_sem, recv_sem, device):
    copy = pltpu.make_async_remote_copy(
        src_ref=source,
        dst_ref=target,
        send_sem=send_sem,
        recv_sem=recv_sem,
        device_id=device,
        device_id_type=MESH,
    )
    copy.start()
    return copy


def exchange_kernel(axes, sizes, active, gather, x_ref, o_ref, send_sem, recv_sem):
    def body():
        me, others = partners(axes, sizes)
        greet(others)
        copies = [
            send(
                x_ref if gather else x_ref.at[index],
                o_ref.at[me],
                send_sem.at[k],
                recv_sem.at[k],
                device,
            )
            for k, (index, device) in enumerate(others)
        ]
        o_ref[me] = x_ref[...] if gather else x_ref[me]
        for copy in copies:
            copy.wait()

    when_active(active, body)


def reduce_kernel(axes, sizes, active, count, *refs):
    parts, sums, landed = refs[:count], refs[count : 2 * count], refs[2 * count : 3 * count]
    send_sem, recv_sem = refs[3 * count :]

    def body():
        me, others = partners(axes, sizes)
        greet(others)
        first = [
            [
                send(
                    parts[a].at[index],
                    landed[a].at[k],
                    send_sem.at[0, a, k],
                    recv_sem.at[0, a, k],
                    device,
                )
                for k, (index, device) in enumerate(others)
            ]
            for a in range(count)
        ]
        second = []
        for a in range(count):
            for copy in first[a]:
                copy.wait()
            total = parts[a][me].astype(F32)
            for k in range(len(others)):
                total = total + landed[a][k].astype(F32)
            sums[a][me] = total.astype(sums[a].dtype)
            for k, (_, device) in enumerate(others):
                second.append(
                    send(
                        sums[a].at[me],
                        sums[a].at[me],
                        send_sem.at[1, a, k],
                        recv_sem.at[1, a, k],
                        device,
                    )
                )
        for copy in second:
            copy.wait()

    when_active(active, body)


class Links:
    def __init__(self):
        self.ids = itertools.count()

    def call(self, kernel, name, out_shape, scratch_shapes, operands):
        in_vmem = pl.BlockSpec(memory_space=pltpu.VMEM)
        return pl.pallas_call(
            kernel,
            out_shape=out_shape,
            in_specs=[in_vmem] * len(operands),
            out_specs=[in_vmem] * len(out_shape),
            scratch_shapes=scratch_shapes,
            compiler_params=pltpu.CompilerParams(
                collective_id=next(self.ids), has_side_effects=True
            ),
            name=name,
        )(*operands)

    def exchange(self, blocks, axes, active, gather=False):
        sizes = [lax.axis_size(axis) for axis in axes]
        members = 1
        for size in sizes:
            members *= size
        shape = (members,) + blocks.shape if gather else blocks.shape
        sems = pltpu.SemaphoreType.DMA((members - 1,))
        return self.call(
            functools.partial(exchange_kernel, axes, sizes, active, gather),
            "gather" if gather else "exchange",
            [jax.ShapeDtypeStruct(shape, blocks.dtype)],
            [sems, sems],
            [blocks],
        )[0]

    def all_sum(self, arrays, axes, active):
        sizes = [lax.axis_size(axis) for axis in axes]
        members = arrays[0].shape[0]
        sems = pltpu.SemaphoreType.DMA((2, len(arrays), members - 1))
        return self.call(
            functools.partial(reduce_kernel, axes, sizes, active, len(arrays)),
            "all_sum",
            [jax.ShapeDtypeStruct(a.shape, a.dtype) for a in arrays],
            [pltpu.VMEM((members - 1,) + a.shape[1:], a.dtype) for a in arrays] + [sems, sems],
            arrays,
        )

    def sum_rows(self, partial_rows, axis, active):
        rows, width = partial_rows.shape
        members = lax.axis_size(axis)
        chunk = -(-rows // (members * ROW_TILE)) * ROW_TILE
        padded = jnp.pad(partial_rows.astype(BF16), ((0, members * chunk - rows), (0, 0)))
        total = self.all_sum([padded.reshape(members, chunk, width)], (axis,), active)[0]
        return total.reshape(members * chunk, width)[:rows].astype(F32)

    def join_columns(self, columns, active):
        rows, width = columns.shape
        pieces = self.exchange(columns.astype(BF16), ("tensor",), active, gather=True)
        return jnp.concatenate([pieces[k] for k in range(pieces.shape[0])], axis=1).astype(F32)


def gelu_value(pre_act):
    inner_arg = GELU_FACTOR * (pre_act + CUBIC_TERM * pre_act * pre_act * pre_act)
    return 0.5 * pre_act * (1.0 + jnp.tanh(inner_arg))


def gelu_slope(pre_act):
    tangent = jnp.tanh(GELU_FACTOR * (pre_act + CUBIC_TERM * pre_act * pre_act * pre_act))
    return 0.5 * (1.0 + tangent) + 0.5 * pre_act * (1.0 - tangent * tangent) * GELU_FACTOR * (
        1.0 + 3.0 * CUBIC_TERM * pre_act * pre_act
    )


def layer_norm(values, scale_row, shift_row):
    average = jnp.mean(values, axis=-1, keepdims=True)
    centred = values - average
    variance = jnp.mean(centred * centred, axis=-1, keepdims=True)
    inv_std = lax.rsqrt(variance + NORM_EPSILON)
    normed = centred * inv_std
    return (normed * scale_row + shift_row, normed, inv_std)


def norm_back(grad_normed, normed, inv_std, scale_row):
    scaled = grad_normed * scale_row
    return (
        scaled
        - jnp.mean(scaled, axis=-1, keepdims=True)
        - normed * jnp.mean(scaled * normed, axis=-1, keepdims=True)
    ) * inv_std


def slot_table(route_rows, experts, capacity):
    flat_ids = route_rows.reshape(-1)
    onehot = (flat_ids[:, None] == jnp.arange(experts, dtype=jnp.int32)[None, :]).astype(jnp.int32)
    before = jnp.cumsum(onehot, axis=0) - onehot
    position = jnp.sum(before * onehot, axis=1)
    return flat_ids * capacity + position


def slot_count(row_count, experts):
    return max(2, (3 * TOPK * row_count + 2 * experts - 1) // (2 * experts))


def attend(query_rows, key_rows, value_rows):
    scores = jnp.einsum(
        "ishe,ithe->ihst", query_rows, key_rows, preferred_element_type=jnp.float32
    ) * HEAD_DIM ** (-0.5)
    log_total = jnp.log(jnp.sum(jnp.exp(scores), axis=-1))
    prob_rows = jnp.exp(scores - log_total[..., None]).astype(jnp.bfloat16)
    attn_mixed = jnp.einsum(
        "ihst,ithe->ishe", prob_rows, value_rows, preferred_element_type=jnp.float32
    ).astype(jnp.bfloat16)
    return (attn_mixed, log_total)


def attend_back(query_rows, key_rows, value_rows, attn_mixed, log_total, grad_mixed):
    scale_factor = HEAD_DIM ** (-0.5)
    scores = (
        jnp.einsum("ishe,ithe->ihst", query_rows, key_rows, preferred_element_type=jnp.float32)
        * scale_factor
    )
    prob_f = jnp.exp(scores - log_total[..., None])
    prob_rows = prob_f.astype(jnp.bfloat16)
    grad_values = jnp.einsum(
        "ihst,ishe->ithe", prob_rows, grad_mixed, preferred_element_type=jnp.float32
    )
    grad_probs = jnp.einsum(
        "ishe,ithe->ihst", grad_mixed, value_rows, preferred_element_type=jnp.float32
    )
    row_delta = jnp.einsum(
        "ishe,ishe->ihs", grad_mixed, attn_mixed, preferred_element_type=jnp.float32
    )
    grad_scores = (prob_f * (grad_probs - row_delta[..., None]) * scale_factor).astype(jnp.bfloat16)
    grad_query = jnp.einsum(
        "ihst,ithe->ishe", grad_scores, key_rows, preferred_element_type=jnp.float32
    )
    grad_keys = jnp.einsum(
        "ihst,ishe->ithe", grad_scores, query_rows, preferred_element_type=jnp.float32
    )
    return (grad_query, grad_keys, grad_values)


def column_parts(rows, weight, experts, transposed):
    members = lax.axis_size("tensor")
    count = rows.shape[0]
    if transposed:
        width = weight.shape[0] // members
        parts = [
            lax.dot_general(
                rows,
                weight[k * width : (k + 1) * width],
                (((1,), (1,)), ((), ())),
                preferred_element_type=F32,
            )
            for k in range(members)
        ]
    else:
        width = weight.shape[1] // members
        parts = [
            jnp.dot(rows, weight[:, k * width : (k + 1) * width], preferred_element_type=F32)
            for k in range(members)
        ]
    return parts, (members * experts, count // experts, width)


def forward_block(links, active, inputs, weights, picks, gate_rows):
    (
        norm_scale,
        norm_shift,
        proj_weight,
        proj_bias,
        attn_weight,
        attn_bias,
        expert_in,
        expert_in_bias,
        expert_out,
        expert_out_bias,
    ) = weights
    row_count, model_width = inputs.shape
    images = row_count // SEQ
    local_width = proj_weight.shape[2]
    head_shape = (images, SEQ, local_width // HEAD_DIM, HEAD_DIM)
    experts = lax.axis_size("expert")
    members = lax.axis_size("tensor")
    slots = picks.shape[2]
    capacity = slots // experts
    normed_out, normed_first, inv_first = layer_norm(inputs, norm_scale[0], norm_shift[0])
    normed_a = normed_out.astype(BF16)
    query_rows, key_rows, value_rows = [
        jnp.dot(normed_a, proj_weight[:, k], preferred_element_type=F32) for k in range(3)
    ]
    query_rows = (query_rows + proj_bias[0]).astype(BF16).reshape(head_shape)
    key_rows = key_rows.astype(BF16).reshape(head_shape)
    value_rows = (value_rows + proj_bias[1]).astype(BF16).reshape(head_shape)
    attn_mixed, log_total = attend(query_rows, key_rows, value_rows)
    partial_value = jnp.dot(
        attn_mixed.reshape(row_count, local_width), attn_weight, preferred_element_type=F32
    )
    hidden_res = inputs + (links.sum_rows(partial_value, "tensor", active) + attn_bias)
    normed_out_b, normed_second, inv_second = layer_norm(hidden_res, norm_scale[1], norm_shift[1])
    outgoing = lax.dot_general(
        picks[0] + picks[1],
        normed_out_b.astype(BF16),
        (((0,), (0,)), ((), ())),
        preferred_element_type=F32,
    ).astype(BF16)
    received = links.exchange(
        outgoing.reshape(experts, capacity, model_width), ("expert",), active
    ).reshape(slots, model_width)
    pre_act = jnp.dot(received, expert_in, preferred_element_type=F32) + expert_in_bias
    activated = gelu_value(pre_act).astype(BF16)
    parts, part_shape = column_parts(activated, expert_out, experts, False)
    width = part_shape[2]
    own_bias = jnp.where(lax.axis_index("tensor") == 0, expert_out_bias, 0.0)
    parts = jnp.stack(
        [
            (part + own_bias[k * width : (k + 1) * width]).astype(BF16)
            for k, part in enumerate(parts)
        ]
    ).reshape(part_shape)
    landed = links.exchange(parts, ("tensor", "expert"), active)
    summed = jnp.sum(landed.reshape(members, slots, width).astype(F32), axis=0).astype(BF16)
    picked = jnp.einsum("jrn,nc->jrc", picks, summed, preferred_element_type=F32)
    branch = gate_rows[:, 0:1] * picked[0] + gate_rows[:, 1:2] * picked[1]
    block_out = hidden_res + links.join_columns(branch, active)
    kept_state = (
        normed_first,
        inv_first,
        normed_a,
        query_rows,
        key_rows,
        value_rows,
        attn_mixed,
        log_total,
        normed_second,
        inv_second,
        received,
        pre_act,
    )
    return (block_out, kept_state)


def backward_block(links, active, cotangent, weights, kept_state, picks, gate_rows):
    (
        norm_scale,
        norm_shift,
        proj_weight,
        proj_bias,
        attn_weight,
        attn_bias,
        expert_in,
        expert_in_bias,
        expert_out,
        expert_out_bias,
    ) = weights
    (
        normed_first,
        inv_first,
        normed_a,
        query_rows,
        key_rows,
        value_rows,
        attn_mixed,
        log_total,
        normed_second,
        inv_second,
        received,
        pre_act,
    ) = kept_state
    row_count, model_width = cotangent.shape
    experts = lax.axis_size("expert")
    members = lax.axis_size("tensor")
    slots = picks.shape[2]
    capacity = slots // experts
    local_width = proj_weight.shape[2]
    grad_rows = jnp.stack([(gate_rows[:, j : j + 1] * cotangent).astype(BF16) for j in range(TOPK)])
    outgoing = jnp.einsum("jrn,jrd->nd", picks, grad_rows, preferred_element_type=F32).astype(BF16)
    grad_out = links.exchange(
        outgoing.reshape(experts, capacity, model_width), ("expert",), active
    ).reshape(slots, model_width)
    grad_pre = lax.dot_general(
        grad_out, expert_out, (((1,), (1,)), ((), ())), preferred_element_type=F32
    ) * gelu_slope(pre_act)
    grad_expert_in_bias = jnp.sum(grad_pre, axis=0)
    grad_pre_b = grad_pre.astype(BF16)
    parts, part_shape = column_parts(grad_pre_b, expert_in, experts, True)
    parts = jnp.stack([part.astype(BF16) for part in parts]).reshape(part_shape)
    landed = links.exchange(parts, ("tensor", "expert"), active)
    summed = jnp.sum(landed.reshape(members, slots, part_shape[2]).astype(F32), axis=0).astype(BF16)
    grad_cols = jnp.dot(picks[0] + picks[1], summed, preferred_element_type=F32)
    grad_normed_b = links.join_columns(grad_cols, active)
    grad_hidden = cotangent + norm_back(grad_normed_b, normed_second, inv_second, norm_scale[1])
    grad_hidden_b = grad_hidden.astype(BF16)
    grad_mixed = (
        lax.dot_general(
            grad_hidden_b, attn_weight, (((1,), (1,)), ((), ())), preferred_element_type=F32
        )
        .astype(BF16)
        .reshape(attn_mixed.shape)
    )
    grad_query, grad_keys, grad_values = attend_back(
        query_rows, key_rows, value_rows, attn_mixed, log_total, grad_mixed
    )
    flats = [g.reshape(row_count, local_width) for g in (grad_query, grad_keys, grad_values)]
    grad_proj_bias = jnp.stack([jnp.sum(flats[0], axis=0), jnp.sum(flats[2], axis=0)])
    grad_proj = [flat.astype(BF16) for flat in flats]
    partial_norm = sum(
        lax.dot_general(
            grad_proj[k], proj_weight[:, k], (((1,), (1,)), ((), ())), preferred_element_type=F32
        )
        for k in range(3)
    )
    grad_normed_a = links.sum_rows(partial_norm, "tensor", active)
    grad_input = grad_hidden + norm_back(grad_normed_a, normed_first, inv_first, norm_scale[0])
    found = (
        grad_out,
        grad_pre_b,
        grad_expert_in_bias,
        grad_normed_b.astype(BF16),
        grad_hidden,
        grad_proj,
        grad_proj_bias,
        grad_normed_a.astype(BF16),
    )
    return (grad_input, found)


def weight_grads(links, kept_state, found):
    normed_first, _, normed_a, _, _, _, attn_mixed, _, normed_second, _, received, pre_act = (
        kept_state
    )
    (
        grad_out,
        grad_pre_b,
        grad_expert_in_bias,
        grad_normed_b,
        grad_hidden,
        grad_proj,
        grad_proj_bias,
        grad_normed_a,
    ) = found
    row_count, model_width = grad_hidden.shape
    experts = lax.axis_size("expert")

    def outer(left, right):
        return lax.dot_general(
            left, right, (((0,), (0,)), ((), ())), preferred_element_type=F32
        )

    grad_attn_bias = jnp.sum(grad_hidden, axis=0)
    grad_attn_weight = outer(attn_mixed.reshape(row_count, -1), grad_hidden.astype(BF16))
    grad_proj_weight = outer(normed_a, jnp.concatenate(grad_proj, axis=1))
    grad_normed_a, grad_normed_b = grad_normed_a.astype(F32), grad_normed_b.astype(F32)
    small = jnp.concatenate(
        [
            jnp.sum(grad_normed_a * normed_first, axis=0),
            jnp.sum(grad_normed_b * normed_second, axis=0),
            jnp.sum(grad_normed_a, axis=0),
            jnp.sum(grad_normed_b, axis=0),
            grad_attn_bias,
            grad_proj_bias.reshape(-1),
        ]
    )
    per_member = -(-small.size // (experts * 128)) * 128
    packed = jnp.pad(small, (0, experts * per_member - small.size)).reshape(experts, 1, per_member)
    proj_sum, attn_sum, small_sum = links.all_sum(
        [
            grad_proj_weight.astype(BF16).reshape(experts, -1, grad_proj_weight.shape[1]),
            grad_attn_weight.astype(BF16).reshape(experts, -1, model_width),
            packed,
        ],
        ("expert",),
        None,
    )
    activated = gelu_value(pre_act).astype(BF16)
    grad_expert_out = outer(activated, grad_out)
    grad_expert_out_bias = jnp.sum(grad_out, axis=0, dtype=F32)
    grad_expert_in = outer(received, grad_pre_b)
    small_sum = small_sum.reshape(-1)
    wide = small_sum[: 5 * model_width].reshape(5, model_width)
    return (
        wide[0:2],
        wide[2:4],
        proj_sum.astype(F32).reshape(model_width, 3, -1),
        small_sum[5 * model_width : small.size].reshape(grad_proj_bias.shape),
        attn_sum.astype(F32).reshape(grad_attn_weight.shape),
        wide[4],
        grad_expert_in[None],
        grad_expert_in_bias[None],
        grad_expert_out[None],
        grad_expert_out_bias[None],
    )


def on_device(
    inputs,
    cotangent,
    norm_scale,
    norm_shift,
    proj_weight,
    proj_bias,
    attn_weight,
    attn_bias,
    expert_in,
    expert_in_bias,
    expert_out,
    expert_out_bias,
    routes,
    gate_weights,
):
    weights = (
        norm_scale[0],
        norm_shift[0],
        proj_weight[0],
        proj_bias[0],
        attn_weight[0],
        attn_bias[0],
        expert_in[0, 0],
        expert_in_bias[0, 0],
        expert_out[0, 0],
        expert_out_bias[0, 0],
    )
    links = Links()
    is_first = lax.axis_index("section") == 0
    experts = lax.axis_size("expert")
    route_rows, gate_rows = routes[0, 0], gate_weights[0, 0]
    row_count = route_rows.shape[0]
    capacity = slot_count(row_count, experts)
    slot_ids = slot_table(route_rows, experts, capacity).reshape(row_count, TOPK)
    picks = (
        slot_ids.T[:, :, None] == jnp.arange(experts * capacity, dtype=jnp.int32)
    ).astype(BF16)

    def by_section(if_first, if_second):
        return jax.tree.map(
            lambda early, late: jnp.where(is_first, early, late), if_first, if_second
        )

    first_out, first_kept = forward_block(links, 0, inputs[0], weights, picks, gate_rows)
    passed_on = from_behind(first_out, "section", 1)
    second_out, second_kept = forward_block(links, 1, passed_on, weights, picks, gate_rows)
    kept_state = by_section(first_kept, second_kept)
    second_grad, second_found = backward_block(
        links, 1, cotangent[0], weights, kept_state, picks, gate_rows
    )
    sent_back = from_behind(second_grad, "section", -1)
    first_grad, first_found = backward_block(
        links, 0, sent_back, weights, kept_state, picks, gate_rows
    )
    found = by_section(first_found, second_found)
    section_out = by_section(first_out, second_out)
    section_in_grad = by_section(first_grad, second_grad)
    grads = weight_grads(links, kept_state, found)
    return (section_out[None, None], section_in_grad[None, None]) + tuple(g[None] for g in grads)


def solution(mesh):
    in_specs = (
        P(None, "expert", None),
        P(None, "expert", None),
        P("section", None, None),
        P("section", None, None),
        P("section", None, None, "tensor"),
        P("section", None, "tensor"),
        P("section", "tensor", None),
        P("section", None),
        P("section", "expert", None, "tensor"),
        P("section", "expert", "tensor"),
        P("section", "expert", "tensor", None),
        P("section", "expert", None),
        P("section", None, "expert", None),
        P("section", None, "expert", None),
    )
    out_specs = (
        P("section", None, "expert", None),
        P("section", None, "expert", None),
        P("section", None, None),
        P("section", None, None),
        P("section", None, None, "tensor"),
        P("section", None, "tensor"),
        P("section", "tensor", None),
        P("section", None),
        P("section", "expert", None, "tensor"),
        P("section", "expert", "tensor"),
        P("section", "expert", "tensor", None),
        P("section", "expert", None),
    )
    return jax.shard_map(
        on_device, mesh=mesh, in_specs=in_specs, out_specs=out_specs, check_vma=False
    )
```

```python
import functools
import itertools

import jax
import jax.numpy as jnp
from jax import lax
from jax.experimental import pallas as pl
from jax.experimental.pallas import tpu as pltpu
from jax.sharding import PartitionSpec as P

HEAD_DIM = 64
SEQ = 197
TOPK = 2


NORM_EPSILON = 1e-06
GELU_FACTOR = 0.7978845608028654
CUBIC_TERM = 0.044715


MESH = pl.DeviceIdType.MESH
ROW_TILE = 16
BF16 = jnp.bfloat16
F32 = jnp.float32


def from_behind(block, axis, distance):
    devices = range(lax.axis_size(axis))
    route = [(i - distance, i) for i in devices if i - distance in devices]
    return lax.ppermute(block, axis, route)


def flat_index(places, sizes):
    total = places[0]
    for place, size in zip(places[1:], sizes[1:]):
        total = total * size + place
    return total


def partners(axes, sizes):
    here = [lax.axis_index(axis) for axis in axes]
    others = []
    for offsets in itertools.product(*[range(size) for size in sizes]):
        if any(offsets):
            there = [
                lax.rem(place + offset, size) if offset else place
                for place, offset, size in zip(here, offsets, sizes)
            ]
            others.append((flat_index(there, sizes), dict(zip(axes, there))))
    return flat_index(here, sizes), others


def greet(others):
    barrier = pltpu.get_barrier_semaphore()
    for _, device in others:
        pl.semaphore_signal(barrier, inc=1, device_id=device, device_id_type=MESH)
    pl.semaphore_wait(barrier, len(others))


def when_active(active, body):
    if active is None:
        body()
    else:
        pl.when(lax.axis_index("section") == active)(body)


def send(source, target, send_sem, recv_sem, device):
    copy = pltpu.make_async_remote_copy(
        src_ref=source,
        dst_ref=target,
        send_sem=send_sem,
        recv_sem=recv_sem,
        device_id=device,
        device_id_type=MESH,
    )
    copy.start()
    return copy


def exchange_kernel(axes, sizes, active, gather, x_ref, o_ref, send_sem, recv_sem):
    def body():
        me, others = partners(axes, sizes)
        greet(others)
        copies = [
            send(
                x_ref if gather else x_ref.at[index],
                o_ref.at[me],
                send_sem.at[k],
                recv_sem.at[k],
                device,
            )
            for k, (index, device) in enumerate(others)
        ]
        o_ref[me] = x_ref[...] if gather else x_ref[me]
        for copy in copies:
            copy.wait()

    when_active(active, body)


def reduce_kernel(axes, sizes, active, count, *refs):
    parts, sums, landed = refs[:count], refs[count : 2 * count], refs[2 * count : 3 * count]
    send_sem, recv_sem = refs[3 * count :]

    def body():
        me, others = partners(axes, sizes)
        greet(others)
        first = [
            [
                send(
                    parts[a].at[index],
                    landed[a].at[k],
                    send_sem.at[0, a, k],
                    recv_sem.at[0, a, k],
                    device,
                )
                for k, (index, device) in enumerate(others)
            ]
            for a in range(count)
        ]
        second = []
        for a in range(count):
            for copy in first[a]:
                copy.wait()
            total = parts[a][me].astype(F32)
            for k in range(len(others)):
                total = total + landed[a][k].astype(F32)
            sums[a][me] = total.astype(sums[a].dtype)
            for k, (_, device) in enumerate(others):
                second.append(
                    send(
                        sums[a].at[me],
                        sums[a].at[me],
                        send_sem.at[1, a, k],
                        recv_sem.at[1, a, k],
                        device,
                    )
                )
        for copy in second:
            copy.wait()

    when_active(active, body)


def mix_kernel(t_sizes, e_sizes, active, *refs):
    (
        part_ref,
        resid_ref,
        rows_ref,
        place_ref,
        received_ref,
        hidden_ref,
        landed,
        total,
        outgoing,
        send_sem,
        recv_sem,
        out_send,
        out_recv,
    ) = refs

    def body():
        me_t, t_others = partners(("tensor",), t_sizes)
        me_e, e_others = partners(("expert",), e_sizes)
        greet(t_others + e_others)
        first = [
            send(part_ref.at[index], landed.at[k], send_sem.at[0, k], recv_sem.at[0, k], device)
            for k, (index, device) in enumerate(t_others)
        ]
        own = part_ref[me_t].astype(F32)
        for k, copy in enumerate(first):
            copy.wait()
            own = own + landed[k].astype(F32)
        total[me_t] = own.astype(BF16)
        second = [
            send(total.at[me_t], total.at[me_t], send_sem.at[1, k], recv_sem.at[1, k], device)
            for k, (_, device) in enumerate(t_others)
        ]
        for copy in second:
            copy.wait()
        rows, width = resid_ref.shape
        mixed = total[...].reshape(-1, width)[:rows].astype(F32)
        hidden = resid_ref[...] + (mixed + rows_ref[0:1])
        hidden_ref[...] = hidden
        normed = layer_norm(hidden, rows_ref[1:2], rows_ref[2:3])[0].astype(BF16)
        third = []
        for k, (index, device) in enumerate(e_others):
            outgoing[index] = jnp.dot(
                place_ref[index], normed, preferred_element_type=F32
            ).astype(BF16)
            third.append(
                send(
                    outgoing.at[index], received_ref.at[me_e], out_send.at[k], out_recv.at[k], device
                )
            )
        received_ref[me_e] = jnp.dot(
            place_ref[me_e], normed, preferred_element_type=F32
        ).astype(BF16)
        for copy in third:
            copy.wait()

    when_active(active, body)


def combine_kernel(sizes, active, *refs):
    part_ref, pick_ref, gate_ref, piece_ref, landed, send_sem, recv_sem, out_send, out_recv = refs

    def body():
        me, others = partners(("tensor", "expert"), sizes)
        me_t, t_others = partners(("tensor",), sizes[:1])
        greet(others)
        first = [
            send(part_ref.at[index], landed.at[me], send_sem.at[k], recv_sem.at[k], device)
            for k, (index, device) in enumerate(others)
        ]
        landed[me] = part_ref[me]
        for copy in first:
            copy.wait()
        members, experts = sizes
        width = landed.shape[2]
        total = landed[0:experts].astype(F32)
        for t in range(1, members):
            total = total + landed[t * experts : (t + 1) * experts].astype(F32)
        total = total.astype(BF16).reshape(-1, width)
        mixed = gate_ref[:, 0:1] * jnp.dot(pick_ref[0], total, preferred_element_type=F32)
        for j in range(1, pick_ref.shape[0]):
            mixed = mixed + gate_ref[:, j : j + 1] * jnp.dot(
                pick_ref[j], total, preferred_element_type=F32
            )
        piece_ref[me_t] = mixed.astype(BF16)
        second = [
            send(piece_ref.at[me_t], piece_ref.at[me_t], out_send.at[k], out_recv.at[k], device)
            for k, (_, device) in enumerate(t_others)
        ]
        for copy in second:
            copy.wait()

    when_active(active, body)


class Links:
    def __init__(self):
        self.ids = itertools.count()

    def call(self, kernel, name, out_shape, scratch_shapes, operands):
        in_vmem = pl.BlockSpec(memory_space=pltpu.VMEM)
        return pl.pallas_call(
            kernel,
            out_shape=out_shape,
            in_specs=[in_vmem] * len(operands),
            out_specs=[in_vmem] * len(out_shape),
            scratch_shapes=scratch_shapes,
            compiler_params=pltpu.CompilerParams(
                collective_id=next(self.ids), has_side_effects=True
            ),
            name=name,
        )(*operands)

    def exchange(self, blocks, axes, active, gather=False):
        sizes = [lax.axis_size(axis) for axis in axes]
        members = 1
        for size in sizes:
            members *= size
        shape = (members,) + blocks.shape if gather else blocks.shape
        sems = pltpu.SemaphoreType.DMA((members - 1,))
        return self.call(
            functools.partial(exchange_kernel, axes, sizes, active, gather),
            "gather" if gather else "exchange",
            [jax.ShapeDtypeStruct(shape, blocks.dtype)],
            [sems, sems],
            [blocks],
        )[0]

    def all_sum(self, arrays, axes, active):
        sizes = [lax.axis_size(axis) for axis in axes]
        members = arrays[0].shape[0]
        sems = pltpu.SemaphoreType.DMA((2, len(arrays), members - 1))
        return self.call(
            functools.partial(reduce_kernel, axes, sizes, active, len(arrays)),
            "all_sum",
            [jax.ShapeDtypeStruct(a.shape, a.dtype) for a in arrays],
            [pltpu.VMEM((members - 1,) + a.shape[1:], a.dtype) for a in arrays] + [sems, sems],
            arrays,
        )

    def row_chunks(self, partial_rows):
        rows, width = partial_rows.shape
        members = lax.axis_size("tensor")
        chunk = -(-rows // (members * ROW_TILE)) * ROW_TILE
        padded = jnp.pad(partial_rows.astype(BF16), ((0, members * chunk - rows), (0, 0)))
        return padded.reshape(members, chunk, width)

    def sum_rows(self, partial_rows, active):
        rows, width = partial_rows.shape
        total = self.all_sum([self.row_chunks(partial_rows)], ("tensor",), active)[0]
        return total.reshape(-1, width)[:rows].astype(F32)

    def mix(self, partial_rows, residual, rows_three, place, active):
        chunks = self.row_chunks(partial_rows)
        members, chunk, width = chunks.shape
        experts, capacity, _ = place.shape
        t_sems = pltpu.SemaphoreType.DMA((2, members - 1))
        e_sems = pltpu.SemaphoreType.DMA((experts - 1,))
        return self.call(
            functools.partial(mix_kernel, [members], [experts], active),
            "mix",
            [
                jax.ShapeDtypeStruct((experts, capacity, width), BF16),
                jax.ShapeDtypeStruct(residual.shape, F32),
            ],
            [
                pltpu.VMEM((members - 1, chunk, width), BF16),
                pltpu.VMEM(chunks.shape, BF16),
                pltpu.VMEM((experts, capacity, width), BF16),
                t_sems,
                t_sems,
                e_sems,
                e_sems,
            ],
            [chunks, residual, rows_three, place],
        )

    def combine(self, parts, picks, gates, active):
        members, experts = lax.axis_size("tensor"), lax.axis_size("expert")
        rows, width = picks.shape[1], parts.shape[2]
        group = pltpu.SemaphoreType.DMA((members * experts - 1,))
        t_sems = pltpu.SemaphoreType.DMA((members - 1,))
        pieces = self.call(
            functools.partial(combine_kernel, [members, experts], active),
            "combine",
            [jax.ShapeDtypeStruct((members, rows, width), BF16)],
            [pltpu.VMEM(parts.shape, BF16), group, group, t_sems, t_sems],
            [parts, picks, gates],
        )[0]
        return jnp.concatenate([pieces[k] for k in range(members)], axis=1).astype(F32)


def gelu_value(pre_act):
    inner_arg = GELU_FACTOR * (pre_act + CUBIC_TERM * pre_act * pre_act * pre_act)
    return 0.5 * pre_act * (1.0 + jnp.tanh(inner_arg))


def gelu_slope(pre_act):
    tangent = jnp.tanh(GELU_FACTOR * (pre_act + CUBIC_TERM * pre_act * pre_act * pre_act))
    return 0.5 * (1.0 + tangent) + 0.5 * pre_act * (1.0 - tangent * tangent) * GELU_FACTOR * (
        1.0 + 3.0 * CUBIC_TERM * pre_act * pre_act
    )


def layer_norm(values, scale_row, shift_row):
    average = jnp.mean(values, axis=-1, keepdims=True)
    centred = values - average
    variance = jnp.mean(centred * centred, axis=-1, keepdims=True)
    inv_std = lax.rsqrt(variance + NORM_EPSILON)
    normed = centred * inv_std
    return (normed * scale_row + shift_row, normed, inv_std)


def norm_back(grad_normed, normed, inv_std, scale_row):
    scaled = grad_normed * scale_row
    return (
        scaled
        - jnp.mean(scaled, axis=-1, keepdims=True)
        - normed * jnp.mean(scaled * normed, axis=-1, keepdims=True)
    ) * inv_std


def slot_table(route_rows, experts, capacity):
    flat_ids = route_rows.reshape(-1)
    onehot = (flat_ids[:, None] == jnp.arange(experts, dtype=jnp.int32)[None, :]).astype(jnp.int32)
    before = jnp.cumsum(onehot, axis=0) - onehot
    position = jnp.sum(before * onehot, axis=1)
    return flat_ids * capacity + position


def slot_count(row_count, experts):
    return max(2, (3 * TOPK * row_count + 2 * experts - 1) // (2 * experts))


def attend(query_rows, key_rows, value_rows):
    scores = jnp.einsum(
        "ishe,ithe->ihst", query_rows, key_rows, preferred_element_type=jnp.float32
    ) * HEAD_DIM ** (-0.5)
    log_total = jnp.log(jnp.sum(jnp.exp(scores), axis=-1))
    prob_rows = jnp.exp(scores - log_total[..., None]).astype(jnp.bfloat16)
    attn_mixed = jnp.einsum(
        "ihst,ithe->ishe", prob_rows, value_rows, preferred_element_type=jnp.float32
    ).astype(jnp.bfloat16)
    return (attn_mixed, log_total)


def attend_back(query_rows, key_rows, value_rows, attn_mixed, log_total, grad_mixed):
    scale_factor = HEAD_DIM ** (-0.5)
    scores = (
        jnp.einsum("ishe,ithe->ihst", query_rows, key_rows, preferred_element_type=jnp.float32)
        * scale_factor
    )
    prob_f = jnp.exp(scores - log_total[..., None])
    prob_rows = prob_f.astype(jnp.bfloat16)
    grad_values = jnp.einsum(
        "ihst,ishe->ithe", prob_rows, grad_mixed, preferred_element_type=jnp.float32
    )
    grad_probs = jnp.einsum(
        "ishe,ithe->ihst", grad_mixed, value_rows, preferred_element_type=jnp.float32
    )
    row_delta = jnp.einsum(
        "ishe,ishe->ihs", grad_mixed, attn_mixed, preferred_element_type=jnp.float32
    )
    grad_scores = (prob_f * (grad_probs - row_delta[..., None]) * scale_factor).astype(jnp.bfloat16)
    grad_query = jnp.einsum(
        "ihst,ithe->ishe", grad_scores, key_rows, preferred_element_type=jnp.float32
    )
    grad_keys = jnp.einsum(
        "ihst,ishe->ithe", grad_scores, query_rows, preferred_element_type=jnp.float32
    )
    return (grad_query, grad_keys, grad_values)


def column_parts(rows, weight, experts, transposed):
    members = lax.axis_size("tensor")
    count = rows.shape[0]
    if transposed:
        width = weight.shape[0] // members
        parts = [
            lax.dot_general(
                rows,
                weight[k * width : (k + 1) * width],
                (((1,), (1,)), ((), ())),
                preferred_element_type=F32,
            )
            for k in range(members)
        ]
    else:
        width = weight.shape[1] // members
        parts = [
            jnp.dot(rows, weight[:, k * width : (k + 1) * width], preferred_element_type=F32)
            for k in range(members)
        ]
    return parts, (members * experts, count // experts, width)


def forward_block(links, active, inputs, weights, picks, place, gate_rows):
    (
        norm_scale,
        norm_shift,
        proj_weight,
        proj_bias,
        attn_weight,
        attn_bias,
        expert_in,
        expert_in_bias,
        expert_out,
        expert_out_bias,
    ) = weights
    row_count, model_width = inputs.shape
    images = row_count // SEQ
    local_width = proj_weight.shape[2]
    head_shape = (images, SEQ, local_width // HEAD_DIM, HEAD_DIM)
    experts = lax.axis_size("expert")
    slots = picks.shape[2]
    normed_out, normed_first, inv_first = layer_norm(inputs, norm_scale[0], norm_shift[0])
    normed_a = normed_out.astype(BF16)
    query_rows, key_rows, value_rows = [
        jnp.dot(normed_a, proj_weight[:, k], preferred_element_type=F32) for k in range(3)
    ]
    query_rows = (query_rows + proj_bias[0]).astype(BF16).reshape(head_shape)
    key_rows = key_rows.astype(BF16).reshape(head_shape)
    value_rows = (value_rows + proj_bias[1]).astype(BF16).reshape(head_shape)
    attn_mixed, log_total = attend(query_rows, key_rows, value_rows)
    partial_value = jnp.dot(
        attn_mixed.reshape(row_count, local_width), attn_weight, preferred_element_type=F32
    )
    rows_three = jnp.stack([attn_bias, norm_scale[1], norm_shift[1]])
    received, hidden_res = links.mix(partial_value, inputs, rows_three, place, active)
    received = received.reshape(slots, model_width)
    _, normed_second, inv_second = layer_norm(hidden_res, norm_scale[1], norm_shift[1])
    pre_act = jnp.dot(received, expert_in, preferred_element_type=F32) + expert_in_bias
    activated = gelu_value(pre_act).astype(BF16)
    parts, part_shape = column_parts(activated, expert_out, experts, False)
    width = part_shape[2]
    own_bias = jnp.where(lax.axis_index("tensor") == 0, expert_out_bias, 0.0)
    parts = jnp.stack(
        [
            (part + own_bias[k * width : (k + 1) * width]).astype(BF16)
            for k, part in enumerate(parts)
        ]
    ).reshape(part_shape)
    block_out = hidden_res + links.combine(parts, picks, gate_rows, active)
    kept_state = (
        normed_first,
        inv_first,
        normed_a,
        query_rows,
        key_rows,
        value_rows,
        attn_mixed,
        log_total,
        normed_second,
        inv_second,
        received,
        pre_act,
    )
    return (block_out, kept_state)


def backward_block(links, active, cotangent, weights, kept_state, picks, gate_rows):
    (
        norm_scale,
        norm_shift,
        proj_weight,
        proj_bias,
        attn_weight,
        attn_bias,
        expert_in,
        expert_in_bias,
        expert_out,
        expert_out_bias,
    ) = weights
    (
        normed_first,
        inv_first,
        normed_a,
        query_rows,
        key_rows,
        value_rows,
        attn_mixed,
        log_total,
        normed_second,
        inv_second,
        received,
        pre_act,
    ) = kept_state
    row_count, model_width = cotangent.shape
    experts = lax.axis_size("expert")
    slots = picks.shape[2]
    capacity = slots // experts
    local_width = proj_weight.shape[2]
    grad_rows = jnp.stack([(gate_rows[:, j : j + 1] * cotangent).astype(BF16) for j in range(TOPK)])
    outgoing = jnp.einsum("jrn,jrd->nd", picks, grad_rows, preferred_element_type=F32).astype(BF16)
    grad_out = links.exchange(
        outgoing.reshape(experts, capacity, model_width), ("expert",), active
    ).reshape(slots, model_width)
    grad_pre = lax.dot_general(
        grad_out, expert_out, (((1,), (1,)), ((), ())), preferred_element_type=F32
    ) * gelu_slope(pre_act)
    grad_expert_in_bias = jnp.sum(grad_pre, axis=0)
    grad_pre_b = grad_pre.astype(BF16)
    parts, part_shape = column_parts(grad_pre_b, expert_in, experts, True)
    parts = jnp.stack([part.astype(BF16) for part in parts]).reshape(part_shape)
    grad_normed_b = links.combine(parts, picks, jnp.ones_like(gate_rows), active)
    grad_hidden = cotangent + norm_back(grad_normed_b, normed_second, inv_second, norm_scale[1])
    grad_hidden_b = grad_hidden.astype(BF16)
    grad_mixed = (
        lax.dot_general(
            grad_hidden_b, attn_weight, (((1,), (1,)), ((), ())), preferred_element_type=F32
        )
        .astype(BF16)
        .reshape(attn_mixed.shape)
    )
    grad_query, grad_keys, grad_values = attend_back(
        query_rows, key_rows, value_rows, attn_mixed, log_total, grad_mixed
    )
    flats = [g.reshape(row_count, local_width) for g in (grad_query, grad_keys, grad_values)]
    grad_proj_bias = jnp.stack([jnp.sum(flats[0], axis=0), jnp.sum(flats[2], axis=0)])
    grad_proj = [flat.astype(BF16) for flat in flats]
    partial_norm = sum(
        lax.dot_general(
            grad_proj[k], proj_weight[:, k], (((1,), (1,)), ((), ())), preferred_element_type=F32
        )
        for k in range(3)
    )
    grad_normed_a = links.sum_rows(partial_norm, active)
    grad_input = grad_hidden + norm_back(grad_normed_a, normed_first, inv_first, norm_scale[0])
    found = (
        grad_out,
        grad_pre_b,
        grad_expert_in_bias,
        grad_normed_b,
        grad_hidden,
        grad_proj,
        grad_proj_bias,
        grad_normed_a,
    )
    return (grad_input, found)


def outer(left, right):
    return lax.dot_general(left, right, (((0,), (0,)), ((), ())), preferred_element_type=F32)


def mixer_sums(links, active, kept_state, found):
    normed_first, _, normed_a, _, _, _, attn_mixed, _, normed_second, _, _, _ = kept_state
    _, _, _, grad_normed_b, grad_hidden, grad_proj, grad_proj_bias, grad_normed_a = found
    row_count, model_width = grad_hidden.shape
    experts = lax.axis_size("expert")
    grad_attn_weight = outer(attn_mixed.reshape(row_count, -1), grad_hidden.astype(BF16))
    grad_proj_weight = outer(normed_a, jnp.concatenate(grad_proj, axis=1))
    small = jnp.concatenate(
        [
            jnp.sum(grad_normed_a * normed_first, axis=0),
            jnp.sum(grad_normed_b * normed_second, axis=0),
            jnp.sum(grad_normed_a, axis=0),
            jnp.sum(grad_normed_b, axis=0),
            jnp.sum(grad_hidden, axis=0),
            grad_proj_bias.reshape(-1),
        ]
    )
    per_member = -(-small.size // (experts * 128)) * 128
    packed = jnp.pad(small, (0, experts * per_member - small.size)).reshape(experts, 1, per_member)
    return links.all_sum(
        [
            grad_proj_weight.astype(BF16).reshape(experts, -1, grad_proj_weight.shape[1]),
            grad_attn_weight.astype(BF16).reshape(experts, -1, model_width),
            packed,
        ],
        ("expert",),
        active,
    )


def weight_grads(sums, local_width, kept_state, found):
    received, pre_act = kept_state[-2:]
    grad_out, grad_pre_b, grad_expert_in_bias = found
    proj_sum, attn_sum, small_sum = sums
    model_width = attn_sum.shape[2]
    activated = gelu_value(pre_act).astype(BF16)
    grad_expert_out = outer(activated, grad_out)
    grad_expert_out_bias = jnp.sum(grad_out, axis=0, dtype=F32)
    grad_expert_in = outer(received, grad_pre_b)
    small_sum = small_sum.reshape(-1)
    wide = small_sum[: 5 * model_width].reshape(5, model_width)
    return (
        wide[0:2],
        wide[2:4],
        proj_sum.astype(F32).reshape(model_width, 3, local_width),
        small_sum[5 * model_width : 5 * model_width + 2 * local_width].reshape(2, local_width),
        attn_sum.astype(F32).reshape(local_width, model_width),
        wide[4],
        grad_expert_in[None],
        grad_expert_in_bias[None],
        grad_expert_out[None],
        grad_expert_out_bias[None],
    )


def on_device(
    inputs,
    cotangent,
    norm_scale,
    norm_shift,
    proj_weight,
    proj_bias,
    attn_weight,
    attn_bias,
    expert_in,
    expert_in_bias,
    expert_out,
    expert_out_bias,
    routes,
    gate_weights,
):
    weights = (
        norm_scale[0],
        norm_shift[0],
        proj_weight[0],
        proj_bias[0],
        attn_weight[0],
        attn_bias[0],
        expert_in[0, 0],
        expert_in_bias[0, 0],
        expert_out[0, 0],
        expert_out_bias[0, 0],
    )
    links = Links()
    is_first = lax.axis_index("section") == 0
    experts = lax.axis_size("expert")
    route_rows, gate_rows = routes[0, 0], gate_weights[0, 0]
    row_count = route_rows.shape[0]
    capacity = -(-slot_count(row_count, experts) // ROW_TILE) * ROW_TILE
    slot_ids = slot_table(route_rows, experts, capacity).reshape(row_count, TOPK)
    picks = (
        slot_ids.T[:, :, None] == jnp.arange(experts * capacity, dtype=jnp.int32)
    ).astype(BF16)

    place = jnp.transpose(
        (picks[0] + picks[1]).reshape(row_count, experts, capacity), (1, 2, 0)
    )

    def by_section(if_first, if_second):
        return jax.tree.map(
            lambda early, late: jnp.where(is_first, early, late), if_first, if_second
        )

    first_out, first_kept = forward_block(links, 0, inputs[0], weights, picks, place, gate_rows)
    passed_on = from_behind(first_out, "section", 1)
    second_out, second_kept = forward_block(links, 1, passed_on, weights, picks, place, gate_rows)
    kept_state = by_section(first_kept, second_kept)
    second_grad, second_found = backward_block(
        links, 1, cotangent[0], weights, kept_state, picks, gate_rows
    )
    sent_back = from_behind(second_grad, "section", -1)
    second_sums = mixer_sums(links, 1, kept_state, second_found)
    sent_back, second_sums = lax.optimization_barrier((sent_back, second_sums))
    first_grad, first_found = backward_block(
        links, 0, sent_back, weights, kept_state, picks, gate_rows
    )
    first_sums = mixer_sums(links, 0, kept_state, first_found)
    found = by_section(first_found[:3], second_found[:3])
    sums = by_section(first_sums, second_sums)
    section_out = by_section(first_out, second_out)
    section_in_grad = by_section(first_grad, second_grad)
    grads = weight_grads(sums, proj_weight.shape[3], kept_state, found)
    return (section_out[None, None], section_in_grad[None, None]) + tuple(g[None] for g in grads)


def solution(mesh):
    in_specs = (
        P(None, "expert", None),
        P(None, "expert", None),
        P("section", None, None),
        P("section", None, None),
        P("section", None, None, "tensor"),
        P("section", None, "tensor"),
        P("section", "tensor", None),
        P("section", None),
        P("section", "expert", None, "tensor"),
        P("section", "expert", "tensor"),
        P("section", "expert", "tensor", None),
        P("section", "expert", None),
        P("section", None, "expert", None),
        P("section", None, "expert", None),
    )
    out_specs = (
        P("section", None, "expert", None),
        P("section", None, "expert", None),
        P("section", None, None),
        P("section", None, None),
        P("section", None, None, "tensor"),
        P("section", None, "tensor"),
        P("section", "tensor", None),
        P("section", None),
        P("section", "expert", None, "tensor"),
        P("section", "expert", "tensor"),
        P("section", "expert", "tensor", None),
        P("section", "expert", None),
    )
    return jax.shard_map(
        on_device, mesh=mesh, in_specs=in_specs, out_specs=out_specs, check_vma=False
    )
```

```python
import functools
import itertools

import jax
import jax.numpy as jnp
from jax import lax
from jax.experimental import pallas as pl
from jax.experimental.pallas import tpu as pltpu
from jax.sharding import PartitionSpec as P

HEAD_DIM = 64
SEQ = 197
TOPK = 2


NORM_EPSILON = 1e-06
GELU_FACTOR = 0.7978845608028654
CUBIC_TERM = 0.044715


MESH = pl.DeviceIdType.MESH
ROW_TILE = 16
BF16 = jnp.bfloat16
F32 = jnp.float32


def from_behind(block, axis, distance):
    devices = range(lax.axis_size(axis))
    route = [(i - distance, i) for i in devices if i - distance in devices]
    return lax.ppermute(block, axis, route)


def flat_index(places, sizes):
    total = places[0]
    for place, size in zip(places[1:], sizes[1:]):
        total = total * size + place
    return total


def partners(axes, sizes):
    here = [lax.axis_index(axis) for axis in axes]
    others = []
    for offsets in itertools.product(*[range(size) for size in sizes]):
        if any(offsets):
            there = [
                lax.rem(place + offset, size) if offset else place
                for place, offset, size in zip(here, offsets, sizes)
            ]
            others.append((flat_index(there, sizes), dict(zip(axes, there))))
    return flat_index(here, sizes), others


def greet(others):
    barrier = pltpu.get_barrier_semaphore()
    for _, device in others:
        pl.semaphore_signal(barrier, inc=1, device_id=device, device_id_type=MESH)
    pl.semaphore_wait(barrier, len(others))


def when_active(active, body):
    if active is None:
        body()
    else:
        pl.when(lax.axis_index("section") == active)(body)


def send(source, target, send_sem, recv_sem, device):
    copy = pltpu.make_async_remote_copy(
        src_ref=source,
        dst_ref=target,
        send_sem=send_sem,
        recv_sem=recv_sem,
        device_id=device,
        device_id_type=MESH,
    )
    copy.start()
    return copy


def exchange_kernel(axes, sizes, active, gather, x_ref, o_ref, send_sem, recv_sem):
    def body():
        me, others = partners(axes, sizes)
        greet(others)
        copies = [
            send(
                x_ref if gather else x_ref.at[index],
                o_ref.at[me],
                send_sem.at[k],
                recv_sem.at[k],
                device,
            )
            for k, (index, device) in enumerate(others)
        ]
        o_ref[me] = x_ref[...] if gather else x_ref[me]
        for copy in copies:
            copy.wait()

    when_active(active, body)


def reduce_kernel(axes, sizes, active, count, *refs):
    parts, sums, landed = refs[:count], refs[count : 2 * count], refs[2 * count : 3 * count]
    send_sem, recv_sem = refs[3 * count :]

    def body():
        me, others = partners(axes, sizes)
        greet(others)
        first = [
            [
                send(
                    parts[a].at[index],
                    landed[a].at[k],
                    send_sem.at[0, a, k],
                    recv_sem.at[0, a, k],
                    device,
                )
                for k, (index, device) in enumerate(others)
            ]
            for a in range(count)
        ]
        second = []
        for a in range(count):
            for copy in first[a]:
                copy.wait()
            total = parts[a][me].astype(F32)
            for k in range(len(others)):
                total = total + landed[a][k].astype(F32)
            sums[a][me] = total.astype(sums[a].dtype)
            for k, (_, device) in enumerate(others):
                second.append(
                    send(
                        sums[a].at[me],
                        sums[a].at[me],
                        send_sem.at[1, a, k],
                        recv_sem.at[1, a, k],
                        device,
                    )
                )
        for copy in second:
            copy.wait()

    when_active(active, body)


def mix_kernel(t_sizes, e_sizes, active, *refs):
    (
        part_ref,
        resid_ref,
        rows_ref,
        place_ref,
        received_ref,
        hidden_ref,
        landed,
        total,
        outgoing,
        send_sem,
        recv_sem,
        out_send,
        out_recv,
    ) = refs

    def body():
        me_t, t_others = partners(("tensor",), t_sizes)
        me_e, e_others = partners(("expert",), e_sizes)
        greet(t_others + e_others)
        first = [
            send(part_ref.at[index], landed.at[k], send_sem.at[0, k], recv_sem.at[0, k], device)
            for k, (index, device) in enumerate(t_others)
        ]
        own = part_ref[me_t].astype(F32)
        for k, copy in enumerate(first):
            copy.wait()
            own = own + landed[k].astype(F32)
        total[me_t] = own.astype(BF16)
        second = [
            send(total.at[me_t], total.at[me_t], send_sem.at[1, k], recv_sem.at[1, k], device)
            for k, (_, device) in enumerate(t_others)
        ]
        for copy in second:
            copy.wait()
        rows, width = resid_ref.shape
        mixed = total[...].reshape(-1, width)[:rows].astype(F32)
        hidden = resid_ref[...] + (mixed + rows_ref[0:1])
        hidden_ref[...] = hidden
        normed = layer_norm(hidden, rows_ref[1:2], rows_ref[2:3])[0].astype(BF16)
        third = []
        for k, (index, device) in enumerate(e_others):
            outgoing[index] = jnp.dot(
                place_ref[index], normed, preferred_element_type=F32
            ).astype(BF16)
            third.append(
                send(
                    outgoing.at[index], received_ref.at[me_e], out_send.at[k], out_recv.at[k], device
                )
            )
        received_ref[me_e] = jnp.dot(
            place_ref[me_e], normed, preferred_element_type=F32
        ).astype(BF16)
        for copy in third:
            copy.wait()

    when_active(active, body)


def combine_kernel(sizes, active, *refs):
    part_ref, pick_ref, gate_ref, piece_ref, landed, send_sem, recv_sem, out_send, out_recv = refs

    def body():
        me, others = partners(("tensor", "expert"), sizes)
        me_t, t_others = partners(("tensor",), sizes[:1])
        greet(others)
        first = [
            send(part_ref.at[index], landed.at[me], send_sem.at[k], recv_sem.at[k], device)
            for k, (index, device) in enumerate(others)
        ]
        landed[me] = part_ref[me]
        for copy in first:
            copy.wait()
        members, experts = sizes
        width = landed.shape[2]
        total = landed[0:experts].astype(F32)
        for t in range(1, members):
            total = total + landed[t * experts : (t + 1) * experts].astype(F32)
        total = total.astype(BF16).reshape(-1, width)
        mixed = gate_ref[:, 0:1] * jnp.dot(pick_ref[0], total, preferred_element_type=F32)
        for j in range(1, pick_ref.shape[0]):
            mixed = mixed + gate_ref[:, j : j + 1] * jnp.dot(
                pick_ref[j], total, preferred_element_type=F32
            )
        piece_ref[me_t] = mixed.astype(BF16)
        second = [
            send(piece_ref.at[me_t], piece_ref.at[me_t], out_send.at[k], out_recv.at[k], device)
            for k, (_, device) in enumerate(t_others)
        ]
        for copy in second:
            copy.wait()

    when_active(active, body)


class Links:
    def __init__(self):
        self.ids = itertools.count()

    def call(self, kernel, name, out_shape, scratch_shapes, operands):
        in_vmem = pl.BlockSpec(memory_space=pltpu.VMEM)
        return pl.pallas_call(
            kernel,
            out_shape=out_shape,
            in_specs=[in_vmem] * len(operands),
            out_specs=[in_vmem] * len(out_shape),
            scratch_shapes=scratch_shapes,
            compiler_params=pltpu.CompilerParams(
                collective_id=next(self.ids), has_side_effects=True
            ),
            name=name,
        )(*operands)

    def exchange(self, blocks, axes, active, gather=False):
        sizes = [lax.axis_size(axis) for axis in axes]
        members = 1
        for size in sizes:
            members *= size
        shape = (members,) + blocks.shape if gather else blocks.shape
        sems = pltpu.SemaphoreType.DMA((members - 1,))
        return self.call(
            functools.partial(exchange_kernel, axes, sizes, active, gather),
            "gather" if gather else "exchange",
            [jax.ShapeDtypeStruct(shape, blocks.dtype)],
            [sems, sems],
            [blocks],
        )[0]

    def all_sum(self, arrays, axes, active):
        sizes = [lax.axis_size(axis) for axis in axes]
        members = arrays[0].shape[0]
        sems = pltpu.SemaphoreType.DMA((2, len(arrays), members - 1))
        return self.call(
            functools.partial(reduce_kernel, axes, sizes, active, len(arrays)),
            "all_sum",
            [jax.ShapeDtypeStruct(a.shape, a.dtype) for a in arrays],
            [pltpu.VMEM((members - 1,) + a.shape[1:], a.dtype) for a in arrays] + [sems, sems],
            arrays,
        )

    def row_chunks(self, partial_rows):
        rows, width = partial_rows.shape
        members = lax.axis_size("tensor")
        chunk = -(-rows // (members * ROW_TILE)) * ROW_TILE
        padded = jnp.pad(partial_rows.astype(BF16), ((0, members * chunk - rows), (0, 0)))
        return padded.reshape(members, chunk, width)

    def sum_rows(self, partial_rows, active):
        rows, width = partial_rows.shape
        total = self.all_sum([self.row_chunks(partial_rows)], ("tensor",), active)[0]
        return total.reshape(-1, width)[:rows].astype(F32)

    def mix(self, partial_rows, residual, rows_three, place, active):
        chunks = self.row_chunks(partial_rows)
        members, chunk, width = chunks.shape
        experts, capacity, _ = place.shape
        t_sems = pltpu.SemaphoreType.DMA((2, members - 1))
        e_sems = pltpu.SemaphoreType.DMA((experts - 1,))
        return self.call(
            functools.partial(mix_kernel, [members], [experts], active),
            "mix",
            [
                jax.ShapeDtypeStruct((experts, capacity, width), BF16),
                jax.ShapeDtypeStruct(residual.shape, F32),
            ],
            [
                pltpu.VMEM((members - 1, chunk, width), BF16),
                pltpu.VMEM(chunks.shape, BF16),
                pltpu.VMEM((experts, capacity, width), BF16),
                t_sems,
                t_sems,
                e_sems,
                e_sems,
            ],
            [chunks, residual, rows_three, place],
        )

    def combine(self, parts, picks, gates, active):
        members, experts = lax.axis_size("tensor"), lax.axis_size("expert")
        rows, width = picks.shape[1], parts.shape[2]
        group = pltpu.SemaphoreType.DMA((members * experts - 1,))
        t_sems = pltpu.SemaphoreType.DMA((members - 1,))
        pieces = self.call(
            functools.partial(combine_kernel, [members, experts], active),
            "combine",
            [jax.ShapeDtypeStruct((members, rows, width), BF16)],
            [pltpu.VMEM(parts.shape, BF16), group, group, t_sems, t_sems],
            [parts, picks, gates],
        )[0]
        return jnp.concatenate([pieces[k] for k in range(members)], axis=1).astype(F32)


def gelu_value(pre_act):
    inner_arg = GELU_FACTOR * (pre_act + CUBIC_TERM * pre_act * pre_act * pre_act)
    return 0.5 * pre_act * (1.0 + jnp.tanh(inner_arg))


def gelu_slope(pre_act):
    tangent = jnp.tanh(GELU_FACTOR * (pre_act + CUBIC_TERM * pre_act * pre_act * pre_act))
    return 0.5 * (1.0 + tangent) + 0.5 * pre_act * (1.0 - tangent * tangent) * GELU_FACTOR * (
        1.0 + 3.0 * CUBIC_TERM * pre_act * pre_act
    )


def layer_norm(values, scale_row, shift_row):
    average = jnp.mean(values, axis=-1, keepdims=True)
    centred = values - average
    variance = jnp.mean(centred * centred, axis=-1, keepdims=True)
    inv_std = lax.rsqrt(variance + NORM_EPSILON)
    normed = centred * inv_std
    return (normed * scale_row + shift_row, normed, inv_std)


def norm_back(grad_normed, normed, inv_std, scale_row):
    scaled = grad_normed * scale_row
    return (
        scaled
        - jnp.mean(scaled, axis=-1, keepdims=True)
        - normed * jnp.mean(scaled * normed, axis=-1, keepdims=True)
    ) * inv_std


def slot_table(route_rows, experts, capacity):
    flat_ids = route_rows.reshape(-1)
    onehot = (flat_ids[:, None] == jnp.arange(experts, dtype=jnp.int32)[None, :]).astype(jnp.int32)
    before = jnp.cumsum(onehot, axis=0) - onehot
    position = jnp.sum(before * onehot, axis=1)
    return flat_ids * capacity + position


def slot_count(row_count, experts):
    return max(2, (3 * TOPK * row_count + 2 * experts - 1) // (2 * experts))


def attend(query_rows, key_rows, value_rows):
    scores = jnp.einsum(
        "ishe,ithe->ihst", query_rows, key_rows, preferred_element_type=jnp.float32
    ) * HEAD_DIM ** (-0.5)
    log_total = jnp.log(jnp.sum(jnp.exp(scores), axis=-1))
    prob_rows = jnp.exp(scores - log_total[..., None]).astype(jnp.bfloat16)
    attn_mixed = jnp.einsum(
        "ihst,ithe->ishe", prob_rows, value_rows, preferred_element_type=jnp.float32
    ).astype(jnp.bfloat16)
    return (attn_mixed, log_total)


def attend_back(query_rows, key_rows, value_rows, attn_mixed, log_total, grad_mixed):
    scale_factor = HEAD_DIM ** (-0.5)
    scores = (
        jnp.einsum("ishe,ithe->ihst", query_rows, key_rows, preferred_element_type=jnp.float32)
        * scale_factor
    )
    prob_f = jnp.exp(scores - log_total[..., None])
    prob_rows = prob_f.astype(jnp.bfloat16)
    grad_values = jnp.einsum(
        "ihst,ishe->ithe", prob_rows, grad_mixed, preferred_element_type=jnp.float32
    )
    grad_probs = jnp.einsum(
        "ishe,ithe->ihst", grad_mixed, value_rows, preferred_element_type=jnp.float32
    )
    row_delta = jnp.einsum(
        "ishe,ishe->ihs", grad_mixed, attn_mixed, preferred_element_type=jnp.float32
    )
    grad_scores = (prob_f * (grad_probs - row_delta[..., None]) * scale_factor).astype(jnp.bfloat16)
    grad_query = jnp.einsum(
        "ihst,ithe->ishe", grad_scores, key_rows, preferred_element_type=jnp.float32
    )
    grad_keys = jnp.einsum(
        "ihst,ishe->ithe", grad_scores, query_rows, preferred_element_type=jnp.float32
    )
    return (grad_query, grad_keys, grad_values)


def column_parts(rows, weight, experts, transposed):
    members = lax.axis_size("tensor")
    count = rows.shape[0]
    if transposed:
        width = weight.shape[0] // members
        parts = [
            lax.dot_general(
                rows,
                weight[k * width : (k + 1) * width],
                (((1,), (1,)), ((), ())),
                preferred_element_type=F32,
            )
            for k in range(members)
        ]
    else:
        width = weight.shape[1] // members
        parts = [
            jnp.dot(rows, weight[:, k * width : (k + 1) * width], preferred_element_type=F32)
            for k in range(members)
        ]
    return parts, (members * experts, count // experts, width)


def forward_block(links, active, inputs, weights, picks, place, gate_rows):
    (
        norm_scale,
        norm_shift,
        proj_weight,
        proj_bias,
        attn_weight,
        attn_bias,
        expert_in,
        expert_in_bias,
        expert_out,
        expert_out_bias,
    ) = weights
    row_count, model_width = inputs.shape
    images = row_count // SEQ
    local_width = proj_weight.shape[2]
    head_shape = (images, SEQ, local_width // HEAD_DIM, HEAD_DIM)
    experts = lax.axis_size("expert")
    slots = picks.shape[2]
    normed_out, normed_first, inv_first = layer_norm(inputs, norm_scale[0], norm_shift[0])
    normed_a = normed_out.astype(BF16)
    query_rows, key_rows, value_rows = [
        jnp.dot(normed_a, proj_weight[:, k], preferred_element_type=F32) for k in range(3)
    ]
    query_rows = (query_rows + proj_bias[0]).astype(BF16).reshape(head_shape)
    key_rows = key_rows.astype(BF16).reshape(head_shape)
    value_rows = (value_rows + proj_bias[1]).astype(BF16).reshape(head_shape)
    attn_mixed, log_total = attend(query_rows, key_rows, value_rows)
    partial_value = jnp.dot(
        attn_mixed.reshape(row_count, local_width), attn_weight, preferred_element_type=F32
    )
    rows_three = jnp.stack([attn_bias, norm_scale[1], norm_shift[1]])
    received, hidden_res = links.mix(partial_value, inputs, rows_three, place, active)
    received = received.reshape(slots, model_width)
    _, normed_second, inv_second = layer_norm(hidden_res, norm_scale[1], norm_shift[1])
    pre_act = jnp.dot(received, expert_in, preferred_element_type=F32) + expert_in_bias
    kept_state = (
        normed_first,
        inv_first,
        normed_a,
        query_rows,
        key_rows,
        value_rows,
        attn_mixed,
        log_total,
        normed_second,
        inv_second,
        received,
        pre_act,
    )
    return (hidden_res, kept_state)


def finish_block(links, active, hidden_res, pre_act, weights, picks, gate_rows):
    expert_out, expert_out_bias = weights[-2:]
    experts = lax.axis_size("expert")
    activated = gelu_value(pre_act).astype(BF16)
    parts, part_shape = column_parts(activated, expert_out, experts, False)
    width = part_shape[2]
    own_bias = jnp.where(lax.axis_index("tensor") == 0, expert_out_bias, 0.0)
    parts = jnp.stack(
        [
            (part + own_bias[k * width : (k + 1) * width]).astype(BF16)
            for k, part in enumerate(parts)
        ]
    ).reshape(part_shape)
    return hidden_res + links.combine(parts, picks, gate_rows, active)


def backward_block(links, active, cotangent, weights, kept_state, picks, gate_rows):
    (
        norm_scale,
        norm_shift,
        proj_weight,
        proj_bias,
        attn_weight,
        attn_bias,
        expert_in,
        expert_in_bias,
        expert_out,
        expert_out_bias,
    ) = weights
    (
        normed_first,
        inv_first,
        normed_a,
        query_rows,
        key_rows,
        value_rows,
        attn_mixed,
        log_total,
        normed_second,
        inv_second,
        received,
        pre_act,
    ) = kept_state
    row_count, model_width = cotangent.shape
    experts = lax.axis_size("expert")
    slots = picks.shape[2]
    capacity = slots // experts
    local_width = proj_weight.shape[2]
    grad_rows = jnp.stack([(gate_rows[:, j : j + 1] * cotangent).astype(BF16) for j in range(TOPK)])
    outgoing = jnp.einsum("jrn,jrd->nd", picks, grad_rows, preferred_element_type=F32).astype(BF16)
    grad_out = links.exchange(
        outgoing.reshape(experts, capacity, model_width), ("expert",), active
    ).reshape(slots, model_width)
    grad_pre = lax.dot_general(
        grad_out, expert_out, (((1,), (1,)), ((), ())), preferred_element_type=F32
    ) * gelu_slope(pre_act)
    grad_expert_in_bias = jnp.sum(grad_pre, axis=0)
    grad_pre_b = grad_pre.astype(BF16)
    parts, part_shape = column_parts(grad_pre_b, expert_in, experts, True)
    parts = jnp.stack([part.astype(BF16) for part in parts]).reshape(part_shape)
    grad_normed_b = links.combine(parts, picks, jnp.ones_like(gate_rows), active)
    grad_hidden = cotangent + norm_back(grad_normed_b, normed_second, inv_second, norm_scale[1])
    grad_hidden_b = grad_hidden.astype(BF16)
    grad_mixed = (
        lax.dot_general(
            grad_hidden_b, attn_weight, (((1,), (1,)), ((), ())), preferred_element_type=F32
        )
        .astype(BF16)
        .reshape(attn_mixed.shape)
    )
    grad_query, grad_keys, grad_values = attend_back(
        query_rows, key_rows, value_rows, attn_mixed, log_total, grad_mixed
    )
    flats = [g.reshape(row_count, local_width) for g in (grad_query, grad_keys, grad_values)]
    grad_proj_bias = jnp.stack([jnp.sum(flats[0], axis=0), jnp.sum(flats[2], axis=0)])
    grad_proj = [flat.astype(BF16) for flat in flats]
    partial_norm = sum(
        lax.dot_general(
            grad_proj[k], proj_weight[:, k], (((1,), (1,)), ((), ())), preferred_element_type=F32
        )
        for k in range(3)
    )
    grad_normed_a = links.sum_rows(partial_norm, active)
    grad_input = grad_hidden + norm_back(grad_normed_a, normed_first, inv_first, norm_scale[0])
    found = (
        grad_out,
        grad_pre_b,
        grad_expert_in_bias,
        grad_normed_b,
        grad_hidden,
        grad_proj,
        grad_proj_bias,
        grad_normed_a,
    )
    return (grad_input, found)


def outer(left, right):
    return lax.dot_general(left, right, (((0,), (0,)), ((), ())), preferred_element_type=F32)


def mixer_sums(links, active, kept_state, found):
    normed_first, _, normed_a, _, _, _, attn_mixed, _, normed_second, _, _, _ = kept_state
    _, _, _, grad_normed_b, grad_hidden, grad_proj, grad_proj_bias, grad_normed_a = found
    row_count, model_width = grad_hidden.shape
    experts = lax.axis_size("expert")
    grad_attn_weight = outer(attn_mixed.reshape(row_count, -1), grad_hidden.astype(BF16))
    grad_proj_weight = outer(normed_a, jnp.concatenate(grad_proj, axis=1))
    small = jnp.concatenate(
        [
            jnp.sum(grad_normed_a * normed_first, axis=0),
            jnp.sum(grad_normed_b * normed_second, axis=0),
            jnp.sum(grad_normed_a, axis=0),
            jnp.sum(grad_normed_b, axis=0),
            jnp.sum(grad_hidden, axis=0),
            grad_proj_bias.reshape(-1),
        ]
    )
    per_member = -(-small.size // (experts * 128)) * 128
    packed = jnp.pad(small, (0, experts * per_member - small.size)).reshape(experts, 1, per_member)
    return links.all_sum(
        [
            grad_proj_weight.astype(BF16).reshape(experts, -1, grad_proj_weight.shape[1]),
            grad_attn_weight.astype(BF16).reshape(experts, -1, model_width),
            packed,
        ],
        ("expert",),
        active,
    )


def weight_grads(sums, local_width, kept_state, found):
    received, pre_act = kept_state[-2:]
    grad_out, grad_pre_b, grad_expert_in_bias = found
    proj_sum, attn_sum, small_sum = sums
    model_width = attn_sum.shape[2]
    activated = gelu_value(pre_act).astype(BF16)
    grad_expert_out = outer(activated, grad_out)
    grad_expert_out_bias = jnp.sum(grad_out, axis=0, dtype=F32)
    grad_expert_in = outer(received, grad_pre_b)
    small_sum = small_sum.reshape(-1)
    wide = small_sum[: 5 * model_width].reshape(5, model_width)
    return (
        wide[0:2],
        wide[2:4],
        proj_sum.astype(F32).reshape(model_width, 3, local_width),
        small_sum[5 * model_width : 5 * model_width + 2 * local_width].reshape(2, local_width),
        attn_sum.astype(F32).reshape(local_width, model_width),
        wide[4],
        grad_expert_in[None],
        grad_expert_in_bias[None],
        grad_expert_out[None],
        grad_expert_out_bias[None],
    )


def on_device(
    inputs,
    cotangent,
    norm_scale,
    norm_shift,
    proj_weight,
    proj_bias,
    attn_weight,
    attn_bias,
    expert_in,
    expert_in_bias,
    expert_out,
    expert_out_bias,
    routes,
    gate_weights,
):
    weights = (
        norm_scale[0],
        norm_shift[0],
        proj_weight[0],
        proj_bias[0],
        attn_weight[0],
        attn_bias[0],
        expert_in[0, 0],
        expert_in_bias[0, 0],
        expert_out[0, 0],
        expert_out_bias[0, 0],
    )
    links = Links()
    is_first = lax.axis_index("section") == 0
    experts = lax.axis_size("expert")
    route_rows, gate_rows = routes[0, 0], gate_weights[0, 0]
    row_count = route_rows.shape[0]
    capacity = -(-slot_count(row_count, experts) // ROW_TILE) * ROW_TILE
    slot_ids = slot_table(route_rows, experts, capacity).reshape(row_count, TOPK)
    picks = (
        slot_ids.T[:, :, None] == jnp.arange(experts * capacity, dtype=jnp.int32)
    ).astype(BF16)

    place = jnp.transpose(
        (picks[0] + picks[1]).reshape(row_count, experts, capacity), (1, 2, 0)
    )

    def by_section(if_first, if_second):
        return jax.tree.map(
            lambda early, late: jnp.where(is_first, early, late), if_first, if_second
        )

    first_hidden, first_kept = forward_block(links, 0, inputs[0], weights, picks, place, gate_rows)
    first_out = finish_block(
        links, 0, first_hidden, first_kept[-1], weights, picks, gate_rows
    )
    passed_on = from_behind(first_out, "section", 1)
    second_hidden, second_kept = forward_block(links, 1, passed_on, weights, picks, place, gate_rows)
    kept_state = by_section(first_kept, second_kept)
    second_grad, second_found = backward_block(
        links, 1, cotangent[0], weights, kept_state, picks, gate_rows
    )
    sent_back = from_behind(second_grad, "section", -1)
    late_pre_act, second_hidden, _ = lax.optimization_barrier(
        (kept_state[-1], second_hidden, second_grad)
    )
    second_out = finish_block(links, 1, second_hidden, late_pre_act, weights, picks, gate_rows)
    second_found, second_out = lax.optimization_barrier((second_found, second_out))
    second_sums = mixer_sums(links, 1, kept_state, second_found)
    sent_back, second_sums = lax.optimization_barrier((sent_back, second_sums))
    first_grad, first_found = backward_block(
        links, 0, sent_back, weights, kept_state, picks, gate_rows
    )
    first_sums = mixer_sums(links, 0, kept_state, first_found)
    found = by_section(first_found[:3], second_found[:3])
    sums = by_section(first_sums, second_sums)
    section_out = by_section(first_out, second_out)
    section_in_grad = by_section(first_grad, second_grad)
    grads = weight_grads(sums, proj_weight.shape[3], kept_state, found)
    return (section_out[None, None], section_in_grad[None, None]) + tuple(g[None] for g in grads)


def solution(mesh):
    in_specs = (
        P(None, "expert", None),
        P(None, "expert", None),
        P("section", None, None),
        P("section", None, None),
        P("section", None, None, "tensor"),
        P("section", None, "tensor"),
        P("section", "tensor", None),
        P("section", None),
        P("section", "expert", None, "tensor"),
        P("section", "expert", "tensor"),
        P("section", "expert", "tensor", None),
        P("section", "expert", None),
        P("section", None, "expert", None),
        P("section", None, "expert", None),
    )
    out_specs = (
        P("section", None, "expert", None),
        P("section", None, "expert", None),
        P("section", None, None),
        P("section", None, None),
        P("section", None, None, "tensor"),
        P("section", None, "tensor"),
        P("section", "tensor", None),
        P("section", None),
        P("section", "expert", None, "tensor"),
        P("section", "expert", "tensor"),
        P("section", "expert", "tensor", None),
        P("section", "expert", None),
    )
    return jax.shard_map(
        on_device, mesh=mesh, in_specs=in_specs, out_specs=out_specs, check_vma=False
    )
```
